32 devices in a mesh: echo: 4 (over y, x), space: 8 (over z, core).
Axes of the slice: x: 2, y: 2, z: 4, core: 2. Of those that a mesh axis runs over, the one named last changes fastest.
Arguments:
- coil_images: bfloat16 [2, 8, 16, 64, 256, 256], P(None, None, 'echo', 'space')
- sensitivities: bfloat16 [2, 16, 64, 256, 256], P(None, 'echo', 'space'), may hold values from -0.72 to 0.72
- mask: int32 [64, 256, 256], P('space'), may hold values 0 or 1
- echo_order: int32 [8], replicated, may hold values from 0 to 7, as said below
Outputs:
- field_map: float32 [64, 256, 256], P('space')
- susceptibility: float32 [64, 256, 256], P('space')
The draws below stay inside these ranges and needn't reach their ends.
Inputs may be any that keep to these rules, and one draw needn't show every extreme that they name: echo_order holds every echo number from 0 to 7 exactly once.
All inputs are finite; a program needn't handle non-finite values. No bound on the sum of `mask` on one device may be relied on, other than what follows from the above.
Results may differ from the reference program's by a relative error of at most 0.0003.
Values sent between devices are 32-bit elements; how exact they have to be, the bound alone decides.
A program may use at most 320 MiB of HBM per device.

```python
import math
import jax
import jax.numpy as jnp
from jax import lax

NZ = 64
NX = 256
NY = 256
COILS = 16
ECHOES = 8
ITERS = 2


def coil_maps_draw(key):
    grid_shape = (2, COILS, NZ, NX, NY)
    return 0.18 * jnp.clip(jax.random.normal(key, grid_shape, jnp.float32), -4.0, 4.0)


def slot_echo_draw(key):
    return jax.random.permutation(jax.random.fold_in(key, 3), ECHOES).astype(jnp.int32)


def draw_sensitivities(key, part):
    return coil_maps_draw(jax.random.fold_in(key, 11)).astype(jnp.bfloat16)


def draw_echo_order(key, part):
    return slot_echo_draw(key)


def draw_coil_images(key, part):
    coil_maps = coil_maps_draw(jax.random.fold_in(key, 11))
    slot_echo = slot_echo_draw(key).astype(jnp.float32)
    volume_shape = (NZ, NX, NY)
    depth_pos = jnp.arange(NZ, dtype=jnp.float32) / max(NZ - 1, 1)
    profile = 0.35 * jnp.power(4.0, depth_pos)
    across = jnp.exp(jax.random.uniform(jax.random.fold_in(key, 21), (NX,), jnp.float32, -0.6, 0.6))
    along_rows = jnp.exp(jax.random.uniform(jax.random.fold_in(key, 22), (NY,), jnp.float32, -0.6, 0.6))
    rough = jax.random.uniform(jax.random.fold_in(key, 23), volume_shape, jnp.float32, 0.4, 1.6)
    magnitude = profile[:, None, None] * across[None, :, None] * along_rows[None, None, :] * rough
    increment = jax.random.uniform(jax.random.fold_in(key, 24), volume_shape, jnp.float32, -1.2, 1.2)
    offset = jax.random.uniform(jax.random.fold_in(key, 25), volume_shape, jnp.float32, -math.pi, math.pi)
    noise_key = jax.random.fold_in(key, 26)

    def one_slot(slot):
        echo_angle = offset + (slot_echo[slot] + 1.0) * increment
        true_real = magnitude * jnp.cos(echo_angle)
        true_imag = magnitude * jnp.sin(echo_angle)
        image_real = coil_maps[0] * true_real[None] - coil_maps[1] * true_imag[None]
        image_imag = coil_maps[0] * true_imag[None] + coil_maps[1] * true_real[None]
        slot_key = jax.random.fold_in(noise_key, slot)
        noise_part = 0.25 * jax.random.normal(slot_key, (2, COILS, NZ, NX, NY), jnp.float32)
        return (jnp.stack([image_real, image_imag]) + noise_part).astype(jnp.bfloat16)
    stacked = lax.map(one_slot, jnp.arange(ECHOES, dtype=jnp.int32))
    return jnp.moveaxis(stacked, 0, 1)


def with_ends(entries, rng, smallest, top_value):
    dims = entries.shape
    index_at = [jax.random.randint(jax.random.fold_in(rng, axis), (), 0, dims[axis]) for axis in range(len(dims))]
    entries = entries.at[tuple(index_at)].set(smallest)
    longest = dims.index(max(dims))
    index_at[longest] = (index_at[longest] + 1) % dims[longest]
    return entries.at[tuple(index_at)].set(top_value)


def setup_inputs(seed: int = 0) -> dict:
    arg_keys = jax.random.split(jax.random.key(seed), 5)
    return {
        "coil_images": draw_coil_images(jax.random.fold_in(arg_keys[4], 71), 0),
        "sensitivities": draw_sensitivities(jax.random.fold_in(arg_keys[4], 71), 0),
        "mask": with_ends((jax.random.randint(arg_keys[2], (NZ, NX, NY), 0, 4) < 3).astype(jnp.int32), jax.random.fold_in(arg_keys[2], 1), 0, 1),
        "echo_order": draw_echo_order(jax.random.fold_in(arg_keys[4], 71), 0),
    }


power_floor = 0.5
tikhonov = 0.05


def fit_field(sums_real, sums_imag, coil_power, mask_values, echo_order):
    inverse_power = 1.0 / jnp.maximum(coil_power, power_floor)
    image_real = sums_real * inverse_power[None]
    image_imag = sums_imag * inverse_power[None]
    echo_count = sums_real.shape[0]
    onehot = (echo_order[None, :] == jnp.arange(echo_count, dtype=jnp.int32)[:, None]).astype(jnp.float32)
    ordered_real = jnp.einsum("ks,szxy->kzxy", onehot, image_real, precision=lax.Precision.HIGHEST)
    ordered_imag = jnp.einsum("ks,szxy->kzxy", onehot, image_imag, precision=lax.Precision.HIGHEST)
    numerator = jnp.sum(ordered_real[:-1] * ordered_imag[1:] - ordered_imag[:-1] * ordered_real[1:], axis=0)
    echo_power = ordered_real * ordered_real + ordered_imag * ordered_imag
    denominator = 1.0 + jnp.sum(0.5 * (echo_power[:-1] + echo_power[1:]), axis=0)
    return mask_values.astype(jnp.float32) * numerator / denominator


def signed_frequency(positions, length):
    shifted = jnp.where(positions < length // 2, positions, positions - length)
    return shifted.astype(jnp.float32) / length


def kernel_values(z_index, x_index, y_index, depth_len, rows_len, cols_len):
    freq_z = signed_frequency(z_index, depth_len)[:, None, None]
    freq_x = signed_frequency(x_index, rows_len)[None, :, None]
    freq_y = signed_frequency(y_index, cols_len)[None, None, :]
    anchor = ((z_index[:, None, None] == 0) & (x_index[None, :, None] == 0) & (y_index[None, None, :] == 0)).astype(jnp.float32)
    total = freq_z * freq_z + freq_x * freq_x + freq_y * freq_y
    return 1.0 / 3.0 - freq_z * freq_z / (total + anchor)


def dipole_map(vector, dipole_kernel):
    spectrum = jnp.fft.fftn(vector)
    return jnp.real(jnp.fft.ifftn(dipole_kernel * spectrum)).astype(jnp.float32)


def reference(coil_images, sensitivities, mask, echo_order):
    sens_real = sensitivities[0].astype(jnp.float32)
    sens_imag = sensitivities[1].astype(jnp.float32)
    coil_power = jnp.sum(sens_real * sens_real + sens_imag * sens_imag, axis=0)

    def one_slot(slot):
        images = lax.dynamic_index_in_dim(coil_images, slot, 1, keepdims=False)
        image_real = images[0].astype(jnp.float32)
        image_imag = images[1].astype(jnp.float32)
        part_real = jnp.sum(sens_real * image_real + sens_imag * image_imag, axis=0)
        part_imag = jnp.sum(sens_real * image_imag - sens_imag * image_real, axis=0)
        return jnp.stack([part_real, part_imag])

    coil_sums = lax.map(one_slot, jnp.arange(ECHOES, dtype=jnp.int32))
    field_map = fit_field(coil_sums[:, 0], coil_sums[:, 1], coil_power, mask, echo_order)

    dipole_kernel = kernel_values(jnp.arange(NZ, dtype=jnp.int32), jnp.arange(NX, dtype=jnp.int32), jnp.arange(NY, dtype=jnp.int32), NZ, NX, NY)
    weights = mask.astype(jnp.float32)

    def normal_map(vector):
        return dipole_map(weights * dipole_map(vector, dipole_kernel), dipole_kernel) + tikhonov * vector

    right = dipole_map(weights * field_map, dipole_kernel)
    susceptibility = jnp.zeros_like(right)
    residual = right
    direction = right
    old_norm = jnp.sum(residual * residual)
    for iteration in range(ITERS):
        product_image = normal_map(direction)
        step_size = old_norm / jnp.sum(direction * product_image)
        susceptibility = susceptibility + step_size * direction
        residual = residual - step_size * product_image
        new_norm = jnp.sum(residual * residual)
        direction = residual + (new_norm / old_norm) * direction
        old_norm = new_norm
    return field_map, susceptibility
```

```python
import functools
import math

import jax
import jax.numpy as jnp
import numpy as np
from jax import lax
from jax.experimental import pallas as pl
from jax.experimental.pallas import tpu as pltpu
from jax.sharding import PartitionSpec as P

power_floor = 0.5
tikhonov = 0.05


def coil_kernel(images_ref, sens_ref, out_ref, *, echoes, coils, rows, cols, row_step, col_step):
    def strip(start, col):
        at_rows = pl.ds(start, row_step)
        at_cols = pl.ds(col, col_step)
        sens_real = []
        sens_imag = []
        power = None
        for coil in range(coils):
            real = sens_ref[0, coil, 0, at_rows, at_cols].astype(jnp.float32)
            imag = sens_ref[1, coil, 0, at_rows, at_cols].astype(jnp.float32)
            sens_real.append(real)
            sens_imag.append(imag)
            square = real * real + imag * imag
            power = square if power is None else power + square
        out_ref[0, 2 * echoes, 0, at_rows, at_cols] = power
        for slot in range(echoes):
            total_real = None
            total_imag = None
            for coil in range(coils):
                real = images_ref[0, slot, coil, 0, at_rows, at_cols].astype(jnp.float32)
                imag = images_ref[1, slot, coil, 0, at_rows, at_cols].astype(jnp.float32)
                part_real = sens_real[coil] * real + sens_imag[coil] * imag
                part_imag = sens_real[coil] * imag - sens_imag[coil] * real
                total_real = part_real if total_real is None else total_real + part_real
                total_imag = part_imag if total_imag is None else total_imag + part_imag
            out_ref[0, slot, 0, at_rows, at_cols] = total_real
            out_ref[0, echoes + slot, 0, at_rows, at_cols] = total_imag

    @pl.loop(0, rows // row_step)
    def _(step):
        start = pl.multiple_of(step * row_step, row_step)
        for col in range(0, cols, col_step):
            strip(start, col)


def coil_sums(coil_images, sensitivities, parts, chunk, chunks):
    _, echoes, coils, depth, rows, cols = coil_images.shape
    part_depth = depth // parts
    chunk_rows = rows // chunks
    block_rows = min(64, chunk_rows)
    blocks = chunk_rows // block_rows
    col_step = 128 if cols % 128 == 0 else cols
    kernel = functools.partial(
        coil_kernel,
        echoes=echoes,
        coils=coils,
        rows=block_rows,
        cols=cols,
        row_step=min(16, block_rows),
        col_step=col_step,
    )
    voxels = depth * chunk_rows * cols
    first = chunk * blocks
    return pl.pallas_call(
        kernel,
        grid=(depth, blocks),
        in_specs=[
            pl.BlockSpec(
                (2, echoes, coils, 1, block_rows, cols), lambda z, b: (0, 0, 0, z, first + b, 0)
            ),
            pl.BlockSpec((2, coils, 1, block_rows, cols), lambda z, b: (0, 0, z, first + b, 0)),
        ],
        out_specs=pl.BlockSpec(
            (1, 2 * echoes + 1, 1, block_rows, cols),
            lambda z, b: (z // part_depth, 0, z % part_depth, b, 0),
        ),
        out_shape=jax.ShapeDtypeStruct(
            (parts, 2 * echoes + 1, part_depth, chunk_rows, cols), jnp.float32
        ),
        compiler_params=pltpu.CompilerParams(vmem_limit_bytes=32 << 20),
        cost_estimate=pl.CostEstimate(
            flops=voxels * echoes * coils * 8,
            bytes_accessed=voxels * (4 * coils * (echoes + 1) + 4 * (2 * echoes + 1)),
            transcendentals=0,
        ),
        name="coil_sums",
    )(coil_images, sensitivities)


def fit_kernel(slot_ref, sums_ref, mask_ref, field_ref, *, echoes):
    inverse_power = 1.0 / jnp.maximum(sums_ref[2 * echoes], power_floor)

    def ordered(k):
        slot = slot_ref[k]
        return sums_ref[slot] * inverse_power, sums_ref[echoes + slot] * inverse_power

    real, imag = ordered(0)
    power = real * real + imag * imag
    numerator = jnp.zeros_like(real)
    power_sum = jnp.zeros_like(real)
    for k in range(1, echoes):
        next_real, next_imag = ordered(k)
        next_power = next_real * next_real + next_imag * next_imag
        numerator = numerator + (real * next_imag - imag * next_real)
        power_sum = power_sum + 0.5 * (power + next_power)
        real, imag, power = next_real, next_imag, next_power
    field_ref[...] = mask_ref[...].astype(jnp.float32) * numerator / (1.0 + power_sum)


def fit_field(slot_of, sums, mask):
    fields, depth, rows, cols = sums.shape
    block_rows = min(32, rows)
    voxels = depth * rows * cols
    return pl.pallas_call(
        functools.partial(fit_kernel, echoes=(fields - 1) // 2),
        grid_spec=pltpu.PrefetchScalarGridSpec(
            num_scalar_prefetch=1,
            grid=(depth, rows // block_rows),
            in_specs=[
                pl.BlockSpec((fields, None, block_rows, cols), lambda z, b, s: (0, z, b, 0)),
                pl.BlockSpec((None, block_rows, cols), lambda z, b, s: (z, b, 0)),
            ],
            out_specs=pl.BlockSpec((None, block_rows, cols), lambda z, b, s: (z, b, 0)),
        ),
        out_shape=jax.ShapeDtypeStruct((depth, rows, cols), jnp.float32),
        cost_estimate=pl.CostEstimate(
            flops=voxels * 100, bytes_accessed=voxels * 4 * (fields + 2), transcendentals=0
        ),
        name="fit_field",
    )(slot_of, sums, mask)


def signed_frequency(positions, length):
    shifted = jnp.where(positions < length // 2, positions, positions - length)
    return shifted.astype(jnp.float32) / length


def kernel_values(z_index, x_index, y_index, depth_len, rows_len, cols_len):
    freq_z = signed_frequency(z_index, depth_len)[:, None, None]
    freq_x = signed_frequency(x_index, rows_len)[None, :, None]
    freq_y = signed_frequency(y_index, cols_len)[None, None, :]
    anchor = (
        (z_index[:, None, None] == 0)
        & (x_index[None, :, None] == 0)
        & (y_index[None, None, :] == 0)
    ).astype(jnp.float32)
    total = freq_z * freq_z + freq_x * freq_x + freq_y * freq_y
    return 1.0 / 3.0 - freq_z * freq_z / (total + anchor)


def hartley_table(length):
    index = np.arange(length)
    radians = 2.0 * math.pi / length * (index[:, None] * index[None, :] % length)
    return jnp.asarray(
        ((np.cos(radians) + np.sin(radians)) / math.sqrt(length)).astype(np.float32)
    )


def on_device(coil_images, sensitivities, mask, echo_order):
    depth, rows, cols = mask.shape
    echo_parts = lax.axis_size("echo")
    split = depth % echo_parts == 0
    parts = echo_parts if split else 1
    axes = ("space", "echo") if split else ("space",)
    part_depth = depth // parts
    count = lax.axis_size("space") * parts
    full_depth = depth * lax.axis_size("space")
    pencil_rows = rows // count
    echoes = echo_order.shape[0]

    numbers = jnp.arange(echoes, dtype=jnp.int32)
    slot_of = jnp.sum(
        jnp.where(echo_order[None, :] == numbers[:, None], numbers[None, :], 0), axis=1
    ).astype(jnp.int32)
    own_mask = mask
    if split:
        own_mask = lax.dynamic_slice_in_dim(
            mask, lax.axis_index("echo") * part_depth, part_depth, 0
        )

    chunks = 4
    chunk_rows = rows // chunks
    fields = []
    for chunk in range(chunks):
        sums = coil_sums(coil_images, sensitivities, parts, chunk, chunks)
        if split:
            sums = lax.psum_scatter(sums, "echo", scatter_dimension=0, tiled=True)
        else:
            sums = lax.psum(sums, "echo")
        chunk_mask = lax.slice_in_dim(own_mask, chunk * chunk_rows, (chunk + 1) * chunk_rows, axis=1)
        fields.append(fit_field(slot_of, sums[0], chunk_mask))
    field = jnp.concatenate(fields, axis=1)

    def spread(values):
        return lax.all_gather(values, "echo", axis=0, tiled=True) if split else values

    place = lax.axis_index("space")
    if split:
        place = place * parts + lax.axis_index("echo")
    dipole = kernel_values(
        jnp.arange(full_depth, dtype=jnp.int32),
        place * pencil_rows + jnp.arange(pencil_rows, dtype=jnp.int32),
        jnp.arange(cols, dtype=jnp.int32),
        full_depth,
        rows,
        cols,
    )
    weights = own_mask.astype(jnp.float32)
    table_z = hartley_table(full_depth)
    table_x = hartley_table(rows)
    table_y = hartley_table(cols)
    exact = functools.partial(jnp.einsum, precision=lax.Precision.HIGHEST)

    def forward(values):
        values = exact("zxy,yl->zxl", values, table_y)
        values = exact("zxl,xk->zkl", values, table_x)
        pencils = lax.all_to_all(values, axes, split_axis=1, concat_axis=0, tiled=True)
        return exact("zkl,zm->mkl", pencils, table_z)

    def backward(spectrum):
        pencils = exact("mkl,mz->zkl", spectrum, table_z)
        values = lax.all_to_all(pencils, axes, split_axis=0, concat_axis=1, tiled=True)
        values = exact("zkl,kx->zxl", values, table_x)
        return exact("zxl,ly->zxy", values, table_y)

    field_map = spread(field)
    right_hat = dipole * forward(weights * field)
    filtered = backward(dipole * right_hat)
    masked = weights * filtered
    old_norm, inner = lax.psum(
        (jnp.sum(right_hat * right_hat), jnp.sum(masked * filtered)), axes
    )
    step_first = old_norm / (inner + tikhonov * old_norm)
    image_hat = dipole * forward(masked) + tikhonov * right_hat
    residual_hat = right_hat - step_first * image_hat
    new_norm, cross = lax.psum(
        (jnp.sum(residual_hat * residual_hat), jnp.sum(residual_hat * right_hat)), axes
    )
    ratio = new_norm / old_norm
    filtered_next = backward(dipole * residual_hat) + ratio * filtered
    direction_norm = new_norm + 2.0 * ratio * cross + ratio * ratio * old_norm
    inner_next = lax.psum(jnp.sum(weights * filtered_next * filtered_next), axes)
    step_second = new_norm / (inner_next + tikhonov * direction_norm)
    first_part = spread(backward(right_hat))
    second_part = spread(backward(residual_hat))
    susceptibility = (step_first + step_second * ratio) * first_part + step_second * second_part
    return (field_map, susceptibility)


def solution(mesh):
    placed = (
        P(None, None, "echo", "space", None, None),
        P(None, "echo", "space", None, None),
        P("space", None, None),
        P(),
    )
    return jax.shard_map(
        on_device,
        mesh=mesh,
        in_specs=placed,
        out_specs=(P("space", None, None), P("space", None, None)),
        check_vma=False,
    )
```

```python
import functools
import math

import jax
import jax.numpy as jnp
import numpy as np
from jax import lax
from jax.experimental import pallas as pl
from jax.experimental.pallas import tpu as pltpu
from jax.sharding import PartitionSpec as P

power_floor = 0.5
tikhonov = 0.05


def coil_kernel(place_ref, images_ref, sens_ref, out_ref, *, echoes, coils, rows, cols, row_step, col_step):
    def strip(start, col):
        at_rows = pl.ds(start, row_step)
        at_cols = pl.ds(col, col_step)
        sens_real = []
        sens_imag = []
        power = None
        for coil in range(coils):
            real = sens_ref[0, coil, 0, at_rows, at_cols].astype(jnp.float32)
            imag = sens_ref[1, coil, 0, at_rows, at_cols].astype(jnp.float32)
            sens_real.append(real)
            sens_imag.append(imag)
            square = real * real + imag * imag
            power = square if power is None else power + square
        out_ref[0, 2 * echoes, 0, at_rows, at_cols] = power
        for slot in range(echoes):
            total_real = None
            total_imag = None
            for coil in range(coils):
                real = images_ref[0, slot, coil, 0, at_rows, at_cols].astype(jnp.float32)
                imag = images_ref[1, slot, coil, 0, at_rows, at_cols].astype(jnp.float32)
                part_real = sens_real[coil] * real + sens_imag[coil] * imag
                part_imag = sens_real[coil] * imag - sens_imag[coil] * real
                total_real = part_real if total_real is None else total_real + part_real
                total_imag = part_imag if total_imag is None else total_imag + part_imag
            out_ref[0, slot, 0, at_rows, at_cols] = total_real
            out_ref[0, echoes + slot, 0, at_rows, at_cols] = total_imag

    @pl.loop(0, rows // row_step)
    def _(step):
        start = pl.multiple_of(step * row_step, row_step)
        for col in range(0, cols, col_step):
            strip(start, col)


def coil_sums(coil_images, sensitivities, place, groups, part_depth, chunk, chunks):
    _, echoes, coils, depth, rows, cols = coil_images.shape
    chunk_rows = rows // chunks
    block_rows = min(64, chunk_rows)
    blocks = chunk_rows // block_rows
    col_step = 128 if cols % 128 == 0 else cols
    kernel = functools.partial(
        coil_kernel,
        echoes=echoes,
        coils=coils,
        rows=block_rows,
        cols=cols,
        row_step=min(16, block_rows),
        col_step=col_step,
    )
    parts = len(groups)
    stride = groups[1] - groups[0] if parts > 1 else 0
    voxels = parts * part_depth * chunk_rows * cols
    first = chunk * blocks

    def plane(i, z, place_ref):
        return (place_ref[0] ^ (groups[0] + stride * i)) * part_depth + z

    return pl.pallas_call(
        kernel,
        grid_spec=pltpu.PrefetchScalarGridSpec(
            num_scalar_prefetch=1,
            grid=(parts, part_depth, blocks),
            in_specs=[
                pl.BlockSpec(
                    (2, echoes, coils, 1, block_rows, cols),
                    lambda i, z, b, p: (0, 0, 0, plane(i, z, p), first + b, 0),
                ),
                pl.BlockSpec(
                    (2, coils, 1, block_rows, cols),
                    lambda i, z, b, p: (0, 0, plane(i, z, p), first + b, 0),
                ),
            ],
            out_specs=pl.BlockSpec(
                (1, 2 * echoes + 1, 1, block_rows, cols), lambda i, z, b, p: (i, 0, z, b, 0)
            ),
        ),
        out_shape=jax.ShapeDtypeStruct(
            (parts, 2 * echoes + 1, part_depth, chunk_rows, cols), jnp.float32
        ),
        compiler_params=pltpu.CompilerParams(vmem_limit_bytes=32 << 20),
        cost_estimate=pl.CostEstimate(
            flops=voxels * echoes * coils * 8,
            bytes_accessed=voxels * (4 * coils * (echoes + 1) + 4 * (2 * echoes + 1)),
            transcendentals=0,
        ),
        name="coil_sums",
    )(place, coil_images, sensitivities)


def fit_kernel(slot_ref, *refs, echoes):
    *term_refs, mask_ref, field_ref = refs

    def total(index):
        value = term_refs[0][index]
        for term_ref in term_refs[1:]:
            value = value + term_ref[index]
        return value

    inverse_power = 1.0 / jnp.maximum(total(2 * echoes), power_floor)

    def ordered(k):
        slot = slot_ref[k]
        return total(slot) * inverse_power, total(echoes + slot) * inverse_power

    real, imag = ordered(0)
    power = real * real + imag * imag
    numerator = jnp.zeros_like(real)
    power_sum = jnp.zeros_like(real)
    for k in range(1, echoes):
        next_real, next_imag = ordered(k)
        next_power = next_real * next_real + next_imag * next_imag
        numerator = numerator + (real * next_imag - imag * next_real)
        power_sum = power_sum + 0.5 * (power + next_power)
        real, imag, power = next_real, next_imag, next_power
    field_ref[...] = mask_ref[...].astype(jnp.float32) * numerator / (1.0 + power_sum)


def fit_field(slot_of, terms, mask):
    _, fields, depth, rows, cols = terms[0].shape
    block_rows = min(32, rows)
    voxels = depth * rows * cols
    term_spec = pl.BlockSpec(
        (None, fields, None, block_rows, cols), lambda z, b, s: (0, 0, z, b, 0)
    )
    plane_spec = pl.BlockSpec((None, block_rows, cols), lambda z, b, s: (z, b, 0))
    return pl.pallas_call(
        functools.partial(fit_kernel, echoes=(fields - 1) // 2),
        grid_spec=pltpu.PrefetchScalarGridSpec(
            num_scalar_prefetch=1,
            grid=(depth, rows // block_rows),
            in_specs=[term_spec] * len(terms) + [plane_spec],
            out_specs=plane_spec,
        ),
        out_shape=jax.ShapeDtypeStruct((depth, rows, cols), jnp.float32),
        cost_estimate=pl.CostEstimate(
            flops=voxels * 100,
            bytes_accessed=voxels * 4 * (fields * len(terms) + 2),
            transcendentals=0,
        ),
        name="fit_field",
    )(slot_of, *terms, mask)


def signed_frequency(positions, length):
    shifted = jnp.where(positions < length // 2, positions, positions - length)
    return shifted.astype(jnp.float32) / length


def kernel_values(z_index, x_index, y_index, depth_len, rows_len, cols_len):
    freq_z = signed_frequency(z_index, depth_len)[:, None, None]
    freq_x = signed_frequency(x_index, rows_len)[None, :, None]
    freq_y = signed_frequency(y_index, cols_len)[None, None, :]
    anchor = (
        (z_index[:, None, None] == 0)
        & (x_index[None, :, None] == 0)
        & (y_index[None, None, :] == 0)
    ).astype(jnp.float32)
    total = freq_z * freq_z + freq_x * freq_x + freq_y * freq_y
    return 1.0 / 3.0 - freq_z * freq_z / (total + anchor)


def hartley_table(length):
    index = np.arange(length)
    radians = 2.0 * math.pi / length * (index[:, None] * index[None, :] % length)
    return jnp.asarray(
        ((np.cos(radians) + np.sin(radians)) / math.sqrt(length)).astype(np.float32)
    )


def on_device(coil_images, sensitivities, mask, echo_order):
    depth, rows, cols = mask.shape
    echo_parts = lax.axis_size("echo")
    split = depth % echo_parts == 0
    parts = echo_parts if split else 1
    axes = ("space", "echo") if split else ("space",)
    part_depth = depth // parts
    count = lax.axis_size("space") * parts
    full_depth = depth * lax.axis_size("space")
    pencil_rows = rows // count
    echoes = echo_order.shape[0]

    numbers = jnp.arange(echoes, dtype=jnp.int32)
    slot_of = jnp.sum(
        jnp.where(echo_order[None, :] == numbers[:, None], numbers[None, :], 0), axis=1
    ).astype(jnp.int32)
    own_mask = mask
    if split:
        own_mask = lax.dynamic_slice_in_dim(
            mask, lax.axis_index("echo") * part_depth, part_depth, 0
        )

    chunks = 8
    chunk_rows = rows // chunks
    echo_place = lax.axis_index("echo").astype(jnp.int32).reshape(1)
    origin = jnp.zeros((1,), jnp.int32)
    pairwise = split and echo_parts == 4
    fields = []
    for chunk in range(chunks):
        if pairwise:
            near, far = ((1, 2), (2, 1))[chunk % 2]

            def partner(values, offset):
                return lax.ppermute(values, "echo", [(e, e ^ offset) for e in range(4)])

            place = (part_depth, chunk, chunks)
            sent = coil_sums(coil_images, sensitivities, echo_place, (near, 3), *place)
            arrived = partner(sent, near)
            kept = coil_sums(coil_images, sensitivities, echo_place, (0, far), *place)
            terms = (kept, arrived, partner(kept[1:] + arrived[1:], far))
        else:
            groups = tuple(range(parts))
            sums = coil_sums(
                coil_images, sensitivities, origin, groups, part_depth, chunk, chunks
            )
            if split:
                sums = lax.psum_scatter(sums, "echo", scatter_dimension=0, tiled=True)
            else:
                sums = lax.psum(sums, "echo")
            terms = (sums,)
        chunk_mask = lax.slice_in_dim(own_mask, chunk * chunk_rows, (chunk + 1) * chunk_rows, axis=1)
        fields.append(fit_field(slot_of, terms, chunk_mask))
    field = jnp.concatenate(fields, axis=1)

    def spread(values):
        return lax.all_gather(values, "echo", axis=0, tiled=True) if split else values

    place = lax.axis_index("space")
    if split:
        place = place * parts + lax.axis_index("echo")
    dipole = kernel_values(
        jnp.arange(full_depth, dtype=jnp.int32),
        place * pencil_rows + jnp.arange(pencil_rows, dtype=jnp.int32),
        jnp.arange(cols, dtype=jnp.int32),
        full_depth,
        rows,
        cols,
    )
    weights = own_mask.astype(jnp.float32)
    table_z = hartley_table(full_depth)
    table_x = hartley_table(rows)
    table_y = hartley_table(cols)
    exact = functools.partial(jnp.einsum, precision=lax.Precision.HIGHEST)

    def forward(values):
        values = exact("zxy,yl->zxl", values, table_y)
        values = exact("zxl,xk->zkl", values, table_x)
        pencils = lax.all_to_all(values, axes, split_axis=1, concat_axis=0, tiled=True)
        return exact("zkl,zm->mkl", pencils, table_z)

    def backward(spectrum):
        pencils = exact("mkl,mz->zkl", spectrum, table_z)
        values = lax.all_to_all(pencils, axes, split_axis=0, concat_axis=1, tiled=True)
        values = exact("zkl,kx->zxl", values, table_x)
        return exact("zxl,ly->zxy", values, table_y)

    def totals(*values):
        row = jnp.pad(jnp.stack(values), (0, 128 - len(values)))
        copies = jnp.broadcast_to(row, (count, 1, 128))
        return jnp.sum(
            lax.all_to_all(copies, axes, split_axis=0, concat_axis=0, tiled=True), axis=(0, 1)
        )

    field_map = spread(field)
    right_hat = dipole * forward(weights * field)
    filtered = backward(dipole * right_hat)
    masked = weights * filtered
    sums = totals(jnp.sum(right_hat * right_hat), jnp.sum(masked * filtered))
    old_norm, inner = sums[0], sums[1]
    step_first = old_norm / (inner + tikhonov * old_norm)
    image_hat = dipole * forward(masked) + tikhonov * right_hat
    residual_hat = right_hat - step_first * image_hat
    filtered_next = backward(dipole * residual_hat)
    sums = totals(
        jnp.sum(residual_hat * residual_hat),
        jnp.sum(residual_hat * right_hat),
        jnp.sum(weights * filtered_next * filtered_next),
        jnp.sum(masked * filtered_next),
    )
    new_norm = sums[0]
    ratio = new_norm / old_norm
    direction_norm = new_norm + 2.0 * ratio * sums[1] + ratio * ratio * old_norm
    inner_next = sums[2] + 2.0 * ratio * sums[3] + ratio * ratio * inner
    step_second = new_norm / (inner_next + tikhonov * direction_norm)
    first_part = spread(backward(right_hat))
    second_part = spread(backward(residual_hat))
    susceptibility = (step_first + step_second * ratio) * first_part + step_second * second_part
    return (field_map, susceptibility)


def solution(mesh):
    placed = (
        P(None, None, "echo", "space", None, None),
        P(None, "echo", "space", None, None),
        P("space", None, None),
        P(),
    )
    return jax.shard_map(
        on_device,
        mesh=mesh,
        in_specs=placed,
        out_specs=(P("space", None, None), P("space", None, None)),
        check_vma=False,
    )
```
